128 devices in a mesh: ctx: 32 (over x, z, core), head: 4 (over y).
Axes of the slice: x: 4, y: 4, z: 4, core: 2. Of those that a mesh axis runs over, the one named last changes fastest.
Arguments:
- queries: bfloat16 [16384, 4096], P('ctx', 'head'), may hold values from -200 to 200
- keys_values: bfloat16 [2, 16384, 4096], P(None, 'ctx', 'head'), may hold values from -7 to 7
- w_out: bfloat16 [4096, 4096], P('head'), may hold values from -0.09375 to 0.09375
- doc_index: int32 [16384], replicated, may hold values from 0 to 31, never falling along the last dimension, each value on 1 to 1152 neighbouring positions
Outputs:
- mixed: bfloat16 [16384, 4096], P(('ctx', 'head'))
The draws below stay inside these ranges and needn't reach their ends.
Inputs may be any that keep to these rules, and one draw needn't show every extreme that they name: `doc_index`: ids never fall along the pack; each document is a run of 1 to 1152 tokens and one has exactly 1152.
All inputs are finite; a program needn't handle non-finite values.
Results may differ from the reference program's by a relative error of at most 0.0095.
Values may be sent and summed in bfloat16 or wider, within the bound.
A program may use at most 64 MiB of HBM per device.

```python
import math
import jax
import jax.numpy as jnp
import numpy as np
from jax import lax

HEADS = 32
HD = 128
D = 4096
TOK_DEV = 512
SPAN = 3
TOKENS = 16384
DOCS = 32
DOC_MOST = 1152
N_CTX = 32
N_HEAD = 4


def joint_draw(key):
    base = jax.random.fold_in(key, 7)
    first, second, third = jax.random.split(base, 3)
    width = HEADS * HD
    query_vals = jnp.clip(jax.random.normal(first, (TOKENS, width), jnp.float32), -6.0, 6.0)
    key_vals = jnp.clip(jax.random.normal(second, (TOKENS, width), jnp.float32), -6.0, 6.0)
    value_vals = jnp.clip(jax.random.normal(third, (TOKENS, width), jnp.float32), -6.0, 6.0)
    return (query_vals, jnp.stack([key_vals, value_vals]))


def draw_queries(key, part):
    return joint_draw(key)[0].astype(jnp.bfloat16)


def draw_keys_values(key, part):
    return joint_draw(key)[1].astype(jnp.bfloat16)


def block_scale(stream_key, extent, cuts, least, high):
    def one(dim, parts):
        draws = jax.random.uniform(jax.random.fold_in(jax.random.fold_in(stream_key, 6), dim), (parts,), jnp.float32, least / len(cuts), high / len(cuts))
        return jnp.repeat(jnp.exp(draws), extent[dim] // parts).reshape((-1,) + (1,) * (len(extent) - dim - 1))

    loudness = one(*cuts[0])
    for cut in cuts[1:]:
        loudness = loudness * one(*cut)
    return loudness


def split_up(number_of, total, most, slope):
    loads = [(1 << 20) // math.isqrt(grade ** slope) + 1 for grade in range(2, number_of + 1)]
    rest, given = total - most - (number_of - 1), [1] * (number_of - 1)
    while rest > 0:
        candidates = [i for i in range(number_of - 1) if given[i] < most]
        mass, remaining = sum([loads[i] for i in candidates]), rest
        for i in candidates:
            extra = min(most - given[i], max(1, remaining * loads[i] // mass), rest)
            given[i] = given[i] + extra
            rest = rest - extra
    return np.array([most] + given)


def ragged(key, number_of, total, reach, lean):
    if number_of == 2:
        one = jax.random.randint(key, (), max(1, total - reach), min(reach, total - 1) + 1)
        return jnp.stack([one, total - one])
    tallies = jnp.asarray(split_up(number_of, total, reach, lean), jnp.int32)
    pairs = (number_of - 1) // 2
    donor, taker = tallies[1:1 + 2 * pairs:2], tallies[2:2 + 2 * pairs:2]
    slack = jnp.minimum(donor - 1, reach - taker)
    shifted = jax.random.randint(jax.random.fold_in(key, 1), (pairs,), 0, 1 << 20) % (slack + 1)
    tallies = tallies.at[1:1 + 2 * pairs:2].set(donor - shifted).at[2:2 + 2 * pairs:2].set(taker + shifted)
    return tallies[jax.random.permutation(jax.random.fold_in(key, 2), number_of)]


def gaussian(stream_key, shape, scale, reach, cuts=(), kind=jnp.bfloat16):
    array = scale * jax.random.normal(stream_key, shape, jnp.float32)
    if cuts:
        array = array * block_scale(stream_key, shape, cuts, -0.22, 0.18)
    return jnp.clip(array, -reach, reach).astype(kind)


def setup_inputs(seed: int = 0) -> dict:
    arg_keys = jax.random.split(jax.random.key(seed), 5)
    return {
        "queries": draw_queries(jax.random.fold_in(arg_keys[4], 71), 0),
        "keys_values": draw_keys_values(jax.random.fold_in(arg_keys[4], 71), 0),
        "w_out": gaussian(arg_keys[2], (HEADS * HD, D), (HEADS * HD) ** -0.5, 0.09375, ((0, 4),)),
        "doc_index": jnp.searchsorted(jnp.cumsum(ragged(arg_keys[3], DOCS, TOKENS, DOC_MOST, 1)), jnp.arange(TOKENS), side="right").astype(jnp.int32),
    }


def attend_head(head, query_rows, window_kv, allowed):
    scale = HD ** -0.5
    query_head = lax.dynamic_slice_in_dim(query_rows, head * HD, HD, 1)
    key_head = lax.dynamic_slice_in_dim(window_kv[0], head * HD, HD, 1)
    value_head = lax.dynamic_slice_in_dim(window_kv[1], head * HD, HD, 1)
    raw = lax.dot_general(query_head, key_head, (((1,), (1,)), ((), ())), preferred_element_type=jnp.float32) * scale
    scores = jnp.where(allowed, raw, jnp.float32(-1e30))
    top = jnp.max(scores, axis=1, keepdims=True)
    weights = jnp.exp(scores - top)
    total = jnp.sum(weights, axis=1, keepdims=True)
    probs = weights.astype(jnp.bfloat16)
    summed = jnp.dot(probs, value_head, preferred_element_type=jnp.float32)
    return summed / total


def reference(queries, keys_values, w_out, doc_index):
    pad_rows = SPAN * TOK_DEV
    window = (SPAN + 1) * TOK_DEV
    padded_kv = jnp.concatenate([jnp.zeros((2, pad_rows, HEADS * HD), jnp.bfloat16), keys_values], axis=1)
    padded_docs = jnp.concatenate([jnp.full((pad_rows,), -1, jnp.int32), doc_index.astype(jnp.int32)])
    group_width = HEADS * HD // N_HEAD

    def one_shard(shard):
        first_row = (shard * TOK_DEV).astype(jnp.int32)
        query_rows = lax.dynamic_slice_in_dim(queries, first_row, TOK_DEV, 0)
        query_docs = lax.dynamic_slice_in_dim(doc_index.astype(jnp.int32), first_row, TOK_DEV, 0)
        query_place = first_row + jnp.arange(TOK_DEV, dtype=jnp.int32)
        window_kv = lax.dynamic_slice_in_dim(padded_kv, first_row, window, 1)
        window_docs = lax.dynamic_slice_in_dim(padded_docs, first_row, window, 0)
        key_place = first_row - pad_rows + jnp.arange(window, dtype=jnp.int32)
        allowed = (window_docs[None, :] == query_docs[:, None]) & (key_place[None, :] <= query_place[:, None])
        per_head = lax.map(lambda head: attend_head(head, query_rows, window_kv, allowed), jnp.arange(HEADS, dtype=jnp.int32))
        attended = jnp.transpose(per_head, (1, 0, 2)).reshape(TOK_DEV, HEADS * HD).astype(jnp.bfloat16)
        summed = jnp.zeros((TOK_DEV, D), jnp.float32)
        for group in range(N_HEAD):
            columns = attended[:, group * group_width:(group + 1) * group_width]
            weight_rows = w_out[group * group_width:(group + 1) * group_width]
            part = jnp.dot(columns, weight_rows, preferred_element_type=jnp.float32).astype(jnp.bfloat16)
            summed = summed + lax.optimization_barrier(part).astype(jnp.float32)
        return summed.astype(jnp.bfloat16)

    blocks = lax.map(one_shard, jnp.arange(N_CTX, dtype=jnp.int32))
    return blocks.reshape(TOKENS, D)
```

```python
import jax
import jax.numpy as jnp
from jax import lax
from jax.sharding import PartitionSpec as P

HD = 128
SPAN = 3
DOC_MOST = 1152
CHUNK = 128


def shift_up(x, axis):
    peers = lax.axis_size(axis)
    return lax.ppermute(x, axis, [(i, i + 1) for i in range(peers - 1)])


def rotate(x, axis, by):
    peers = lax.axis_size(axis)
    return lax.ppermute(x, axis, [(i, (i + by) % peers) for i in range(peers)])


def per_device(queries, keys_values, w_out, doc_index):
    rows, width = queries.shape
    heads = width // HD
    groups = lax.axis_size("head")
    me = lax.axis_index("ctx")
    h = lax.axis_index("head")
    first_row = me * rows
    tail = DOC_MOST - 2 * rows
    r1 = shift_up(keys_values, "ctx")
    r2 = shift_up(r1, "ctx")
    r3 = shift_up(r2[:, rows - tail:], "ctx")
    window = jnp.concatenate([r3, r2, r1, keys_values], axis=1)
    padded_docs = jnp.concatenate([jnp.full((DOC_MOST,), -1, jnp.int32), doc_index])
    span = DOC_MOST + CHUNK
    scale = HD ** (-0.5)

    def chunk_part(c):
        start = c * CHUNK
        q = lax.dynamic_slice_in_dim(queries, start, CHUNK, 0).reshape(CHUNK, heads, HD)
        kv = lax.dynamic_slice_in_dim(window, start, span, 1)
        k = kv[0].reshape(span, heads, HD)
        v = kv[1].reshape(span, heads, HD)
        q_docs = lax.dynamic_slice_in_dim(doc_index, first_row + start, CHUNK)
        k_docs = lax.dynamic_slice_in_dim(padded_docs, first_row + start, span)
        q_place = start + jnp.arange(CHUNK, dtype=jnp.int32)
        k_place = start - DOC_MOST + jnp.arange(span, dtype=jnp.int32)
        allowed = (k_docs[None, :] == q_docs[:, None]) & (k_place[None, :] <= q_place[:, None])
        raw = jnp.einsum("qhd,khd->hqk", q, k, preferred_element_type=jnp.float32) * scale
        scores = jnp.where(allowed[None], raw, jnp.float32(-1e30))
        top = jnp.max(scores, axis=2, keepdims=True)
        weights = jnp.exp(scores - top)
        total = jnp.sum(weights, axis=2)
        probs = weights.astype(jnp.bfloat16)
        summed = jnp.einsum("hqk,khd->qhd", probs, v, preferred_element_type=jnp.float32)
        attended = (summed / jnp.transpose(total)[:, :, None]).astype(jnp.bfloat16)
        attended = attended.reshape(CHUNK, heads * HD)
        return jnp.dot(attended, w_out, preferred_element_type=jnp.float32).astype(jnp.bfloat16)

    total_out = None
    for step in range(groups):
        by = (step + 1) % groups
        part = chunk_part((h + by) % groups)
        if by:
            part = rotate(part, "head", by)
        part = part.astype(jnp.float32)
        total_out = part if total_out is None else total_out + part
    return total_out.astype(jnp.bfloat16)


def solution(mesh):
    in_specs = (P("ctx", "head"), P(None, "ctx", "head"), P("head", None), P())
    out_specs = P(("ctx", "head"), None)
    return jax.shard_map(
        per_device, mesh=mesh, in_specs=in_specs, out_specs=out_specs, check_vma=False
    )
```

```python
import jax
import jax.numpy as jnp
from jax import lax
from jax.sharding import PartitionSpec as P

HD = 128
DOC_MOST = 1152
CHUNK = 128


def shift_up(x, axis):
    peers = lax.axis_size(axis)
    return lax.ppermute(x, axis, [(i, i + 1) for i in range(peers - 1)])


def per_device(queries, keys_values, w_out, doc_index):
    rows, width = queries.shape
    heads = width // HD
    groups = lax.axis_size("head")
    chunks = rows // CHUNK
    me = lax.axis_index("ctx")
    h = lax.axis_index("head")
    first_row = me * rows
    back = DOC_MOST // CHUNK
    r1 = shift_up(keys_values, "ctx")
    own_pieces = [keys_values[:, i * CHUNK:(i + 1) * CHUNK] for i in range(chunks)]
    r1_pieces = [r1[:, i * CHUNK:(i + 1) * CHUNK] for i in range(chunks)]
    upper = shift_up(r1[:, rows - 2 * CHUNK:], "ctx")
    r2_pieces = [None] * chunks
    r2_pieces[chunks - 2] = upper[:, :CHUNK]
    r2_pieces[chunks - 1] = upper[:, CHUNK:]
    for i in range(chunks - 3, -1, -1):
        r2_pieces[i] = shift_up(r1_pieces[i], "ctx")
    r3_piece = shift_up(r2_pieces[chunks - 1], "ctx")
    pieces = [r3_piece] + r2_pieces + r1_pieces + own_pieces
    assert len(pieces) == back + chunks
    padded_docs = jnp.concatenate([jnp.full((DOC_MOST,), -1, jnp.int32), doc_index])
    span = DOC_MOST + CHUNK
    scale = HD ** (-0.5)

    def chunk_part(c):
        start = c * CHUNK
        q = queries[start:start + CHUNK].reshape(CHUNK, heads, HD)
        kv = jnp.concatenate(pieces[c:c + back + 1], axis=1)
        k = kv[0].reshape(span, heads, HD)
        v = kv[1].reshape(span, heads, HD)
        q_docs = lax.dynamic_slice_in_dim(doc_index, first_row + start, CHUNK)
        k_docs = lax.dynamic_slice_in_dim(padded_docs, first_row + start, span)
        q_place = start + jnp.arange(CHUNK, dtype=jnp.int32)
        k_place = start - DOC_MOST + jnp.arange(span, dtype=jnp.int32)
        allowed = (k_docs[None, :] == q_docs[:, None]) & (k_place[None, :] <= q_place[:, None])
        raw = jnp.einsum("qhd,khd->hqk", q, k, preferred_element_type=jnp.float32) * scale
        scores = jnp.where(allowed[None], raw, jnp.float32(-1e30))
        top = jnp.max(scores, axis=2, keepdims=True)
        weights = jnp.exp(scores - top)
        total = jnp.sum(weights, axis=2)
        probs = weights.astype(jnp.bfloat16)
        summed = jnp.einsum("hqk,khd->qhd", probs, v, preferred_element_type=jnp.float32)
        attended = (summed / jnp.transpose(total)[:, :, None]).astype(jnp.bfloat16)
        attended = attended.reshape(CHUNK, heads * HD)
        return jnp.dot(attended, w_out, preferred_element_type=jnp.float32).astype(jnp.bfloat16)

    total_out = None
    for c in range(chunks - 1, -1, -1):
        part = chunk_part(c)
        owner = c % groups
        terms = [jnp.where(h == owner, part, jnp.zeros_like(part)).astype(jnp.float32)]
        for by in range(1, groups):
            src = (owner - by) % groups
            got = lax.ppermute(part, "head", [(src, owner)])
            terms.append(got.astype(jnp.float32))
        for t in terms:
            total_out = t if total_out is None else total_out + t
    return total_out.astype(jnp.bfloat16)


def solution(mesh):
    in_specs = (P("ctx", "head"), P(None, "ctx", "head"), P("head", None), P())
    out_specs = P(("ctx", "head"), None)
    return jax.shard_map(
        per_device, mesh=mesh, in_specs=in_specs, out_specs=out_specs, check_vma=False
    )
```

```python
import functools

import jax
import jax.numpy as jnp
from jax import lax
from jax.experimental import pallas as pl
from jax.experimental.pallas import tpu as pltpu
from jax.sharding import PartitionSpec as P

HD = 128
DOC_MOST = 1152
CHUNK = 128
NEG = -1e30


def shift_up(x, axis):
    peers = lax.axis_size(axis)
    return lax.ppermute(x, axis, [(i, i + 1) for i in range(peers - 1)])


def rotate(x, axis, by):
    peers = lax.axis_size(axis)
    return lax.ppermute(x, axis, [(i, (i + by) % peers) for i in range(peers)])


def attend_kernel(heads, steps, sp, q_ref, qdoc_ref, kdoc_ref, tail_ref, win_ref, o_ref, m_sc, l_sc, acc_sc):
    t = pl.program_id(0)
    c = sp[0]
    lo = sp[1]
    kb = c + t

    @pl.when(t == 0)
    def _():
        m_sc[...] = jnp.full_like(m_sc, NEG)
        l_sc[...] = jnp.zeros_like(l_sc)
        acc_sc[...] = jnp.zeros_like(acc_sc)

    def body(kv_ref):
        q_place = c * CHUNK + lax.broadcasted_iota(jnp.int32, (CHUNK, CHUNK), 0)
        k_place = kb * CHUNK - DOC_MOST + lax.broadcasted_iota(jnp.int32, (CHUNK, CHUNK), 1)
        allowed = (kdoc_ref[...] == qdoc_ref[...]) & (k_place <= q_place)
        for hh in range(heads):
            cols = slice(hh * HD, (hh + 1) * HD)
            raw = lax.dot_general(
                q_ref[:, cols], kv_ref[0, :, cols], (((1,), (1,)), ((), ())),
                preferred_element_type=jnp.float32,
            ) * HD ** (-0.5)
            s = jnp.where(allowed, raw, jnp.float32(NEG))
            m_old = m_sc[hh]
            m_new = jnp.maximum(m_old, jnp.max(s, axis=1, keepdims=True))
            alpha = jnp.exp(m_old - m_new)
            p = jnp.exp(s - m_new)
            l_sc[hh] = alpha * l_sc[hh] + jnp.sum(p, axis=1, keepdims=True)
            acc_sc[hh] = alpha * acc_sc[hh] + jnp.dot(
                p.astype(jnp.bfloat16), kv_ref[1, :, cols], preferred_element_type=jnp.float32
            )
            m_sc[hh] = m_new

    @pl.when((kb >= lo) & (kb == 0))
    def _():
        body(tail_ref)

    @pl.when((kb >= lo) & (kb > 0))
    def _():
        body(win_ref)

    @pl.when(t == steps - 1)
    def _():
        for hh in range(heads):
            o_ref[:, hh * HD:(hh + 1) * HD] = (acc_sc[hh] / l_sc[hh]).astype(o_ref.dtype)


def attend_chunk(sp, queries, q_docs, k_docs, tail, window):
    rows, width = queries.shape
    heads = width // HD
    steps = DOC_MOST // CHUNK + 1
    blocks = window.shape[1] // CHUNK

    def win_map(t, sp):
        return (0, jnp.clip(jnp.maximum(sp[0] + t, sp[1]) - 1, 0, blocks - 1), 0)

    def kdoc_map(t, sp):
        return (0, jnp.maximum(sp[0] + t, sp[1]))

    return pl.pallas_call(
        functools.partial(attend_kernel, heads, steps),
        out_shape=jax.ShapeDtypeStruct((CHUNK, width), jnp.bfloat16),
        grid_spec=pltpu.PrefetchScalarGridSpec(
            num_scalar_prefetch=1,
            grid=(steps,),
            in_specs=[
                pl.BlockSpec((CHUNK, width), lambda t, sp: (sp[0], 0)),
                pl.BlockSpec((CHUNK, 1), lambda t, sp: (sp[0], 0)),
                pl.BlockSpec((1, CHUNK), kdoc_map),
                pl.BlockSpec((2, CHUNK, width), lambda t, sp: (0, 0, 0)),
                pl.BlockSpec((2, CHUNK, width), win_map),
            ],
            out_specs=pl.BlockSpec((CHUNK, width), lambda t, sp: (0, 0)),
            scratch_shapes=[
                pltpu.VMEM((heads, CHUNK, 1), jnp.float32),
                pltpu.VMEM((heads, CHUNK, 1), jnp.float32),
                pltpu.VMEM((heads, CHUNK, HD), jnp.float32),
            ],
        ),
        compiler_params=pltpu.CompilerParams(dimension_semantics=("arbitrary",)),
        cost_estimate=pl.CostEstimate(
            flops=4 * CHUNK * (DOC_MOST + CHUNK) * width,
            transcendentals=CHUNK * (DOC_MOST + CHUNK) * heads,
            bytes_accessed=2 * 2 * (DOC_MOST + CHUNK) * width + 4 * CHUNK * width,
        ),
    )(sp, queries, q_docs, k_docs, tail, window)


def per_device(queries, keys_values, w_out, doc_index):
    rows, width = queries.shape
    groups = lax.axis_size("head")
    me = lax.axis_index("ctx")
    h = lax.axis_index("head")
    first_row = me * rows
    tail_rows = DOC_MOST - 2 * rows
    r1 = shift_up(keys_values, "ctx")
    r2 = shift_up(r1, "ctx")
    r3 = shift_up(r2[:, rows - tail_rows:], "ctx")
    window = jnp.concatenate([r2, r1, keys_values], axis=1)
    padded_docs = jnp.concatenate([jnp.full((DOC_MOST,), -1, jnp.int32), doc_index])
    k_docs = lax.dynamic_slice_in_dim(padded_docs, first_row, DOC_MOST + rows).reshape(1, -1)
    q_docs = lax.dynamic_slice_in_dim(doc_index, first_row, rows).reshape(rows, 1)

    total_out = None
    for step in range(groups):
        by = (step + 1) % groups
        c = (h + by) % groups
        first_doc = doc_index[first_row + c * CHUNK]
        doc_start = jnp.sum((doc_index < first_doc).astype(jnp.int32))
        lo = jnp.clip((doc_start - first_row + DOC_MOST) // CHUNK, c, c + DOC_MOST // CHUNK)
        sp = jnp.stack([c, lo]).astype(jnp.int32)
        attended = attend_chunk(sp, queries, q_docs, k_docs, r3, window)
        part = jnp.dot(attended, w_out, preferred_element_type=jnp.float32).astype(jnp.bfloat16)
        if by:
            part = rotate(part, "head", by)
        part = part.astype(jnp.float32)
        total_out = part if total_out is None else total_out + part
    return total_out.astype(jnp.bfloat16)


def solution(mesh):
    in_specs = (P("ctx", "head"), P(None, "ctx", "head"), P("head", None), P())
    out_specs = P(("ctx", "head"), None)
    return jax.shard_map(
        per_device, mesh=mesh, in_specs=in_specs, out_specs=out_specs, check_vma=False
    )
```

```python
import jax
import jax.numpy as jnp
from jax import lax
from jax.sharding import PartitionSpec as P

HD = 128
SPAN = 3
DOC_MOST = 1152
CHUNK = 128


def shift_up(x, axis):
    peers = lax.axis_size(axis)
    return lax.ppermute(x, axis, [(i, i + 1) for i in range(peers - 1)])


def rotate(x, axis, by):
    peers = lax.axis_size(axis)
    return lax.ppermute(x, axis, [(i, (i + by) % peers) for i in range(peers)])


def per_device(queries, keys_values, w_out, doc_index):
    rows, width = queries.shape
    heads = width // HD
    groups = lax.axis_size("head")
    me = lax.axis_index("ctx")
    h = lax.axis_index("head")
    first_row = me * rows
    tail = DOC_MOST - 2 * rows
    r1 = shift_up(keys_values, "ctx")
    r2 = shift_up(r1, "ctx")
    r3 = shift_up(r2[:, rows - tail:], "ctx")
    sources = [r3, r2, r1, keys_values]
    offsets = [-DOC_MOST, -2 * rows, -rows, 0]
    padded_docs = jnp.concatenate([jnp.full((DOC_MOST,), -1, jnp.int32), doc_index])
    scale = HD ** (-0.5)

    def chunk_part(c):
        start = c * CHUNK
        q = lax.dynamic_slice_in_dim(queries, start, CHUNK, 0).reshape(CHUNK, heads, HD)
        q_docs = lax.dynamic_slice_in_dim(doc_index, first_row + start, CHUNK)
        q_place = start + jnp.arange(CHUNK, dtype=jnp.int32)
        score_list = []
        for kv, off in zip(sources, offsets):
            n = kv.shape[1]
            k = kv[0].reshape(n, heads, HD)
            k_docs = lax.dynamic_slice_in_dim(padded_docs, first_row + DOC_MOST + off, n)
            k_place = off + jnp.arange(n, dtype=jnp.int32)
            allowed = (k_docs[None, :] == q_docs[:, None]) & (k_place[None, :] <= q_place[:, None])
            raw = jnp.einsum("qhd,khd->hqk", q, k, preferred_element_type=jnp.float32) * scale
            score_list.append(jnp.where(allowed[None], raw, jnp.float32(-1e30)))
        top = score_list[0].max(axis=2, keepdims=True)
        for s in score_list[1:]:
            top = jnp.maximum(top, s.max(axis=2, keepdims=True))
        total = None
        summed = None
        for kv, s in zip(sources, score_list):
            n = kv.shape[1]
            weights = jnp.exp(s - top)
            t = jnp.sum(weights, axis=2)
            probs = weights.astype(jnp.bfloat16)
            pv = jnp.einsum("hqk,khd->qhd", probs, kv[1].reshape(n, heads, HD), preferred_element_type=jnp.float32)
            total = t if total is None else total + t
            summed = pv if summed is None else summed + pv
        attended = (summed / jnp.transpose(total)[:, :, None]).astype(jnp.bfloat16)
        attended = attended.reshape(CHUNK, heads * HD)
        return jnp.dot(attended, w_out, preferred_element_type=jnp.float32).astype(jnp.bfloat16)

    total_out = None
    for step in range(groups):
        by = (step + 1) % groups
        part = chunk_part((h + by) % groups)
        if by:
            part = rotate(part, "head", by)
        part = part.astype(jnp.float32)
        total_out = part if total_out is None else total_out + part
    return total_out.astype(jnp.bfloat16)


def solution(mesh):
    in_specs = (P("ctx", "head"), P(None, "ctx", "head"), P("head", None), P())
    out_specs = P(("ctx", "head"), None)
    return jax.shard_map(
        per_device, mesh=mesh, in_specs=in_specs, out_specs=out_specs, check_vma=False
    )
```

```python
import jax
import jax.numpy as jnp
from jax import lax
from jax.sharding import PartitionSpec as P

HD = 128
SPAN = 3
DOC_MOST = 1152
CHUNK = 128


def shift_up(x, axis):
    peers = lax.axis_size(axis)
    return lax.ppermute(x, axis, [(i, i + 1) for i in range(peers - 1)])


def rotate(x, axis, by):
    peers = lax.axis_size(axis)
    return lax.ppermute(x, axis, [(i, (i + by) % peers) for i in range(peers)])


def per_device(queries, keys_values, w_out, doc_index):
    rows, width = queries.shape
    heads = width // HD
    groups = lax.axis_size("head")
    me = lax.axis_index("ctx")
    h = lax.axis_index("head")
    first_row = me * rows
    tail = DOC_MOST - 2 * rows
    r1 = shift_up(keys_values, "ctx")
    r2_tail = shift_up(r1[:, rows - tail:], "ctx")
    r3 = shift_up(r2_tail, "ctx")
    r2_head = shift_up(r1[:, :rows - tail], "ctx")
    sources = [r3, r2_head, r2_tail, r1, keys_values]
    offsets = [-DOC_MOST, -2 * rows, -rows - tail, -rows, 0]
    padded_docs = jnp.concatenate([jnp.full((DOC_MOST,), -1, jnp.int32), doc_index])
    scale = HD ** (-0.5)

    def chunk_part(c):
        start = c * CHUNK
        q = lax.dynamic_slice_in_dim(queries, start, CHUNK, 0).reshape(CHUNK, heads, HD)
        q_docs = lax.dynamic_slice_in_dim(doc_index, first_row + start, CHUNK)
        q_place = start + jnp.arange(CHUNK, dtype=jnp.int32)
        score_list = []
        for kv, off in zip(sources, offsets):
            n = kv.shape[1]
            k = kv[0].reshape(n, heads, HD)
            k_docs = lax.dynamic_slice_in_dim(padded_docs, first_row + DOC_MOST + off, n)
            k_place = off + jnp.arange(n, dtype=jnp.int32)
            allowed = (k_docs[None, :] == q_docs[:, None]) & (k_place[None, :] <= q_place[:, None])
            raw = jnp.einsum("qhd,khd->hqk", q, k, preferred_element_type=jnp.float32) * scale
            score_list.append(jnp.where(allowed[None], raw, jnp.float32(-1e30)))
        top = score_list[0].max(axis=2, keepdims=True)
        for s in score_list[1:]:
            top = jnp.maximum(top, s.max(axis=2, keepdims=True))
        total = None
        summed = None
        for kv, s in zip(sources, score_list):
            n = kv.shape[1]
            weights = jnp.exp(s - top)
            t = jnp.sum(weights, axis=2)
            probs = weights.astype(jnp.bfloat16)
            pv = jnp.einsum("hqk,khd->qhd", probs, kv[1].reshape(n, heads, HD), preferred_element_type=jnp.float32)
            total = t if total is None else total + t
            summed = pv if summed is None else summed + pv
        attended = (summed / jnp.transpose(total)[:, :, None]).astype(jnp.bfloat16)
        attended = attended.reshape(CHUNK, heads * HD)
        return jnp.dot(attended, w_out, preferred_element_type=jnp.float32).astype(jnp.bfloat16)

    total_out = None
    for step in range(groups):
        by = (step + 1) % groups
        part = chunk_part((h + by) % groups)
        if by:
            part = rotate(part, "head", by)
        part = part.astype(jnp.float32)
        total_out = part if total_out is None else total_out + part
    return total_out.astype(jnp.bfloat16)


def solution(mesh):
    in_specs = (P("ctx", "head"), P(None, "ctx", "head"), P("head", None), P())
    out_specs = P(("ctx", "head"), None)
    return jax.shard_map(
        per_device, mesh=mesh, in_specs=in_specs, out_specs=out_specs, check_vma=False
    )
```

```python
import jax
import jax.numpy as jnp
from jax import lax
from jax.sharding import PartitionSpec as P

HD = 128
SPAN = 3
DOC_MOST = 1152
CHUNK = 128


def shift_up(x, axis):
    peers = lax.axis_size(axis)
    return lax.ppermute(x, axis, [(i, i + 1) for i in range(peers - 1)])


def rotate(x, axis, by):
    peers = lax.axis_size(axis)
    return lax.ppermute(x, axis, [(i, (i + by) % peers) for i in range(peers)])


def per_device(queries, keys_values, w_out, doc_index):
    rows, width = queries.shape
    heads = width // HD
    groups = lax.axis_size("head")
    me = lax.axis_index("ctx")
    h = lax.axis_index("head")
    first_row = me * rows
    tail = DOC_MOST - 2 * rows
    r1 = shift_up(keys_values, "ctx")
    r2 = shift_up(r1, "ctx")
    r3 = shift_up(r2[:, rows - tail:], "ctx")
    sources = [r3, r2, r1, keys_values]
    offsets = [-DOC_MOST, -2 * rows, -rows, 0]
    padded_docs = jnp.concatenate([jnp.full((DOC_MOST,), -1, jnp.int32), doc_index])
    scale = HD ** (-0.5)

    def chunk_part(c):
        start = c * CHUNK
        q = lax.dynamic_slice_in_dim(queries, start, CHUNK, 0).reshape(CHUNK, heads, HD)
        q_docs = lax.dynamic_slice_in_dim(doc_index, first_row + start, CHUNK)
        q_place = start + jnp.arange(CHUNK, dtype=jnp.int32)
        def scores(kv, off):
            n = kv.shape[1]
            k = kv[0].reshape(n, heads, HD)
            k_docs = lax.dynamic_slice_in_dim(padded_docs, first_row + DOC_MOST + off, n)
            k_place = off + jnp.arange(n, dtype=jnp.int32)
            allowed = (k_docs[None, :] == q_docs[:, None]) & (k_place[None, :] <= q_place[:, None])
            raw = jnp.einsum("qhd,khd->hqk", q, k, preferred_element_type=jnp.float32) * scale
            return jnp.where(allowed[None], raw, jnp.float32(-1e30))

        def stage(pairs, top):
            score_list = [scores(kv, off) for kv, off in pairs]
            for s in score_list:
                top = jnp.maximum(top, s.max(axis=2, keepdims=True))
            total = None
            summed = None
            for (kv, _), s in zip(pairs, score_list):
                n = kv.shape[1]
                weights = jnp.exp(s - top)
                t = jnp.sum(weights, axis=2)
                probs = weights.astype(jnp.bfloat16)
                pv = jnp.einsum("hqk,khd->qhd", probs, kv[1].reshape(n, heads, HD), preferred_element_type=jnp.float32)
                total = t if total is None else total + t
                summed = pv if summed is None else summed + pv
            return top, total, summed

        near = list(zip(sources[2:], offsets[2:]))
        far = list(zip(sources[:2], offsets[:2]))
        floor = jnp.full((heads, CHUNK, 1), -1e30, jnp.float32)
        top_a, total_a, summed_a = stage(near, floor)
        top, total_b, summed_b = stage(far, top_a)
        alpha = jnp.exp(top_a - top)
        total = alpha[:, :, 0] * total_a + total_b
        summed = jnp.transpose(alpha, (1, 0, 2)) * summed_a + summed_b
        attended = (summed / jnp.transpose(total)[:, :, None]).astype(jnp.bfloat16)
        attended = attended.reshape(CHUNK, heads * HD)
        return jnp.dot(attended, w_out, preferred_element_type=jnp.float32).astype(jnp.bfloat16)

    total_out = None
    for step in range(groups):
        by = (step + 1) % groups
        part = chunk_part((h + by) % groups)
        if by:
            part = rotate(part, "head", by)
        part = part.astype(jnp.float32)
        total_out = part if total_out is None else total_out + part
    return total_out.astype(jnp.bfloat16)


def solution(mesh):
    in_specs = (P("ctx", "head"), P(None, "ctx", "head"), P("head", None), P())
    out_specs = P(("ctx", "head"), None)
    return jax.shard_map(
        per_device, mesh=mesh, in_specs=in_specs, out_specs=out_specs, check_vma=False
    )
```

```python
import jax
import jax.numpy as jnp
from jax import lax
from jax.sharding import PartitionSpec as P

HD = 128
SPAN = 3
DOC_MOST = 1152
CHUNK = 128


def shift_up(x, axis):
    peers = lax.axis_size(axis)
    return lax.ppermute(x, axis, [(i, i + 1) for i in range(peers - 1)])


def rotate(x, axis, by):
    peers = lax.axis_size(axis)
    return lax.ppermute(x, axis, [(i, (i + by) % peers) for i in range(peers)])


def per_device(queries, keys_values, w_out, doc_index):
    rows, width = queries.shape
    heads = width // HD
    groups = lax.axis_size("head")
    me = lax.axis_index("ctx")
    h = lax.axis_index("head")
    first_row = me * rows
    tail = DOC_MOST - 2 * rows
    r1 = shift_up(keys_values, "ctx")
    r2 = shift_up(r1, "ctx")
    r3 = shift_up(r2[:, rows - tail:], "ctx")
    sources = [r3, r2, r1, keys_values]
    offsets = [-DOC_MOST, -2 * rows, -rows, 0]
    padded_docs = jnp.concatenate([jnp.full((DOC_MOST,), -1, jnp.int32), doc_index])
    scale = HD ** (-0.5)

    def chunk_part(c):
        start = c * CHUNK
        q = lax.dynamic_slice_in_dim(queries, start, CHUNK, 0).reshape(CHUNK, heads, HD)
        q_docs = lax.dynamic_slice_in_dim(doc_index, first_row + start, CHUNK)
        q_place = start + jnp.arange(CHUNK, dtype=jnp.int32)
        def scores(kv, off):
            n = kv.shape[1]
            k = kv[0].reshape(n, heads, HD)
            k_docs = lax.dynamic_slice_in_dim(padded_docs, first_row + DOC_MOST + off, n)
            k_place = off + jnp.arange(n, dtype=jnp.int32)
            allowed = (k_docs[None, :] == q_docs[:, None]) & (k_place[None, :] <= q_place[:, None])
            raw = jnp.einsum("qhd,khd->hqk", q, k, preferred_element_type=jnp.float32) * scale
            return jnp.where(allowed[None], raw, jnp.float32(-1e30))

        def stage(pairs, top):
            score_list = [scores(kv, off) for kv, off in pairs]
            for s in score_list:
                top = jnp.maximum(top, s.max(axis=2, keepdims=True))
            total = None
            summed = None
            for (kv, _), s in zip(pairs, score_list):
                n = kv.shape[1]
                weights = jnp.exp(s - top)
                t = jnp.sum(weights, axis=2)
                probs = weights.astype(jnp.bfloat16)
                pv = jnp.einsum("hqk,khd->qhd", probs, kv[1].reshape(n, heads, HD), preferred_element_type=jnp.float32)
                total = t if total is None else total + t
                summed = pv if summed is None else summed + pv
            return top, total, summed

        near = list(zip(sources[2:], offsets[2:]))
        far = list(zip(sources[:2], offsets[:2]))
        floor = jnp.full((heads, CHUNK, 1), -1e30, jnp.float32)
        top_a, total_a, summed_a = stage(near, floor)
        top, total_b, summed_b = stage(far, top_a)
        alpha = jnp.exp(top_a - top)
        total = alpha[:, :, 0] * total_a + total_b
        summed = jnp.transpose(alpha, (1, 0, 2)) * summed_a + summed_b
        attended = (summed / jnp.transpose(total)[:, :, None]).astype(jnp.bfloat16)
        attended = attended.reshape(CHUNK, heads * HD)
        return jnp.dot(attended, w_out, preferred_element_type=jnp.float32).astype(jnp.bfloat16)

    assert groups == 4
    cols = w_out.shape[1] // 2
    far = chunk_part((h + 2) % groups)
    via_left = rotate(far[:, :cols], "head", groups - 1)
    via_right = rotate(far[:, cols:], "head", 1)
    nxt = chunk_part((h + 1) % groups)
    nxt = jnp.concatenate(
        [nxt[:, :cols], (nxt[:, cols:].astype(jnp.float32) + via_right.astype(jnp.float32)).astype(jnp.bfloat16)],
        axis=1,
    )
    from_left = rotate(nxt, "head", 1)
    prv = chunk_part((h + groups - 1) % groups)
    prv = jnp.concatenate(
        [(prv[:, :cols].astype(jnp.float32) + via_left.astype(jnp.float32)).astype(jnp.bfloat16), prv[:, cols:]],
        axis=1,
    )
    from_right = rotate(prv, "head", groups - 1)
    own = chunk_part(h)
    total_out = own.astype(jnp.float32) + from_left.astype(jnp.float32) + from_right.astype(jnp.float32)
    return total_out.astype(jnp.bfloat16)


def solution(mesh):
    in_specs = (P("ctx", "head"), P(None, "ctx", "head"), P("head", None), P())
    out_specs = P(("ctx", "head"), None)
    return jax.shard_map(
        per_device, mesh=mesh, in_specs=in_specs, out_specs=out_specs, check_vma=False
    )
```

```python
import jax
import jax.numpy as jnp
from jax import lax
from jax.sharding import PartitionSpec as P

HD = 128
SPAN = 3
DOC_MOST = 1152
CHUNK = 128


def shift_up(x, axis):
    peers = lax.axis_size(axis)
    return lax.ppermute(x, axis, [(i, i + 1) for i in range(peers - 1)])


def rotate(x, axis, by):
    peers = lax.axis_size(axis)
    return lax.ppermute(x, axis, [(i, (i + by) % peers) for i in range(peers)])


def per_device(queries, keys_values, w_out, doc_index):
    rows, width = queries.shape
    heads = width // HD
    groups = lax.axis_size("head")
    me = lax.axis_index("ctx")
    h = lax.axis_index("head")
    first_row = me * rows
    tail = DOC_MOST - 2 * rows
    r1 = shift_up(keys_values, "ctx")
    r2 = shift_up(r1, "ctx")
    r3 = shift_up(r2[:, rows - tail:], "ctx")
    sources = [r3, r2, r1, keys_values]
    offsets = [-DOC_MOST, -2 * rows, -rows, 0]
    padded_docs = jnp.concatenate([jnp.full((DOC_MOST,), -1, jnp.int32), doc_index])
    scale = HD ** (-0.5)

    def chunk_part(c):
        start = c * CHUNK
        q = lax.dynamic_slice_in_dim(queries, start, CHUNK, 0).reshape(CHUNK, heads, HD)
        q_docs = lax.dynamic_slice_in_dim(doc_index, first_row + start, CHUNK)
        q_place = start + jnp.arange(CHUNK, dtype=jnp.int32)
        def scores(kv, off):
            n = kv.shape[1]
            k = kv[0].reshape(n, heads, HD)
            k_docs = lax.dynamic_slice_in_dim(padded_docs, first_row + DOC_MOST + off, n)
            k_place = off + jnp.arange(n, dtype=jnp.int32)
            allowed = (k_docs[None, :] == q_docs[:, None]) & (k_place[None, :] <= q_place[:, None])
            raw = jnp.einsum("qhd,khd->hqk", q, k, preferred_element_type=jnp.float32) * scale
            return jnp.where(allowed[None], raw, jnp.float32(-1e30))

        def stage(pairs, top):
            score_list = [scores(kv, off) for kv, off in pairs]
            for s in score_list:
                top = jnp.maximum(top, s.max(axis=2, keepdims=True))
            total = None
            summed = None
            for (kv, _), s in zip(pairs, score_list):
                n = kv.shape[1]
                weights = jnp.exp(s - top)
                t = jnp.sum(weights, axis=2)
                probs = weights.astype(jnp.bfloat16)
                pv = jnp.einsum("hqk,khd->qhd", probs, kv[1].reshape(n, heads, HD), preferred_element_type=jnp.float32)
                total = t if total is None else total + t
                summed = pv if summed is None else summed + pv
            return top, total, summed

        floor = jnp.full((heads, CHUNK, 1), -1e30, jnp.float32)
        top, total, summed = stage(list(zip(sources[2:], offsets[2:])), floor)
        for kv, off in zip(sources[1::-1], offsets[1::-1]):
            new_top, new_total, new_summed = stage([(kv, off)], top)
            alpha = jnp.exp(top - new_top)
            total = alpha[:, :, 0] * total + new_total
            summed = jnp.transpose(alpha, (1, 0, 2)) * summed + new_summed
            top = new_top
        attended = (summed / jnp.transpose(total)[:, :, None]).astype(jnp.bfloat16)
        attended = attended.reshape(CHUNK, heads * HD)
        return jnp.dot(attended, w_out, preferred_element_type=jnp.float32).astype(jnp.bfloat16)

    assert groups == 4
    cols = w_out.shape[1] // 2
    far = chunk_part((h + 2) % groups)
    via_left = rotate(far[:, :cols], "head", groups - 1)
    via_right = rotate(far[:, cols:], "head", 1)
    nxt = chunk_part((h + 1) % groups)
    nxt = jnp.concatenate(
        [nxt[:, :cols], (nxt[:, cols:].astype(jnp.float32) + via_right.astype(jnp.float32)).astype(jnp.bfloat16)],
        axis=1,
    )
    from_left = rotate(nxt, "head", 1)
    prv = chunk_part((h + groups - 1) % groups)
    prv = jnp.concatenate(
        [(prv[:, :cols].astype(jnp.float32) + via_left.astype(jnp.float32)).astype(jnp.bfloat16), prv[:, cols:]],
        axis=1,
    )
    from_right = rotate(prv, "head", groups - 1)
    own = chunk_part(h)
    total_out = own.astype(jnp.float32) + from_left.astype(jnp.float32) + from_right.astype(jnp.float32)
    return total_out.astype(jnp.bfloat16)


def solution(mesh):
    in_specs = (P("ctx", "head"), P(None, "ctx", "head"), P("head", None), P())
    out_specs = P(("ctx", "head"), None)
    return jax.shard_map(
        per_device, mesh=mesh, in_specs=in_specs, out_specs=out_specs, check_vma=False
    )
```

```python
import jax
import jax.numpy as jnp
from jax import lax
from jax.sharding import PartitionSpec as P

HD = 128
SPAN = 3
DOC_MOST = 1152
CHUNK = 128


def shift_up(x, axis):
    peers = lax.axis_size(axis)
    return lax.ppermute(x, axis, [(i, i + 1) for i in range(peers - 1)])


def rotate(x, axis, by):
    peers = lax.axis_size(axis)
    return lax.ppermute(x, axis, [(i, (i + by) % peers) for i in range(peers)])


def per_device(queries, keys_values, w_out, doc_index):
    rows, width = queries.shape
    heads = width // HD
    groups = lax.axis_size("head")
    me = lax.axis_index("ctx")
    h = lax.axis_index("head")
    first_row = me * rows
    tail = DOC_MOST - 2 * rows
    r1 = shift_up(keys_values, "ctx")
    r2 = shift_up(r1, "ctx")
    r3 = shift_up(r2[:, rows - tail:], "ctx")
    sources = [r3, r2, r1, keys_values]
    offsets = [-DOC_MOST, -2 * rows, -rows, 0]
    padded_docs = jnp.concatenate([jnp.full((DOC_MOST,), -1, jnp.int32), doc_index])
    scale = HD ** (-0.5)

    def chunk_part(c):
        start = c * CHUNK
        q = lax.dynamic_slice_in_dim(queries, start, CHUNK, 0).reshape(CHUNK, heads, HD)
        q_docs = lax.dynamic_slice_in_dim(doc_index, first_row + start, CHUNK)
        q_place = start + jnp.arange(CHUNK, dtype=jnp.int32)
        def scores(kv, off):
            n = kv.shape[1]
            k = kv[0].reshape(n, heads, HD)
            k_docs = lax.dynamic_slice_in_dim(padded_docs, first_row + DOC_MOST + off, n)
            k_place = off + jnp.arange(n, dtype=jnp.int32)
            allowed = (k_docs[None, :] == q_docs[:, None]) & (k_place[None, :] <= q_place[:, None])
            raw = jnp.einsum("qhd,khd->hqk", q, k, preferred_element_type=jnp.float32) * scale
            return jnp.where(allowed[None], raw, jnp.float32(-1e30))

        def stage(pairs, top):
            score_list = [scores(kv, off) for kv, off in pairs]
            for s in score_list:
                top = jnp.maximum(top, s.max(axis=2, keepdims=True))
            total = None
            summed = None
            for (kv, _), s in zip(pairs, score_list):
                n = kv.shape[1]
                weights = jnp.exp(s - top)
                t = jnp.sum(weights, axis=2)
                probs = weights.astype(jnp.bfloat16)
                pv = jnp.einsum("hqk,khd->qhd", probs, kv[1].reshape(n, heads, HD), preferred_element_type=jnp.float32)
                total = t if total is None else total + t
                summed = pv if summed is None else summed + pv
            return top, total, summed

        near = list(zip(sources[2:], offsets[2:]))
        far = list(zip(sources[:2], offsets[:2]))
        floor = jnp.full((heads, CHUNK, 1), -1e30, jnp.float32)
        top_a, total_a, summed_a = stage(near, floor)
        top, total_b, summed_b = stage(far, top_a)
        alpha = jnp.exp(top_a - top)
        total = alpha[:, :, 0] * total_a + total_b
        summed = jnp.transpose(alpha, (1, 0, 2)) * summed_a + summed_b
        attended = (summed / jnp.transpose(total)[:, :, None]).astype(jnp.bfloat16)
        attended = attended.reshape(CHUNK, heads * HD)
        return jnp.dot(attended, w_out, preferred_element_type=jnp.float32).astype(jnp.bfloat16)

    assert groups == 4
    cols = w_out.shape[1] // 2
    far = chunk_part((h + 2) % groups)
    via_left = rotate(far[:, :cols], "head", groups - 1)
    via_right = rotate(far[:, cols:], "head", 1)
    nxt = chunk_part((h + 1) % groups)
    left_of_next = rotate(nxt[:, :cols], "head", 1)
    right_of_next = rotate(
        (nxt[:, cols:].astype(jnp.float32) + via_right.astype(jnp.float32)).astype(jnp.bfloat16), "head", 1
    )
    prv = chunk_part((h + groups - 1) % groups)
    right_of_prev = rotate(prv[:, cols:], "head", groups - 1)
    left_of_prev = rotate(
        (prv[:, :cols].astype(jnp.float32) + via_left.astype(jnp.float32)).astype(jnp.bfloat16), "head", groups - 1
    )
    from_left = jnp.concatenate([left_of_next, right_of_next], axis=1)
    from_right = jnp.concatenate([left_of_prev, right_of_prev], axis=1)
    own = chunk_part(h)
    total_out = own.astype(jnp.float32) + from_left.astype(jnp.float32) + from_right.astype(jnp.float32)
    return total_out.astype(jnp.bfloat16)


def solution(mesh):
    in_specs = (P("ctx", "head"), P(None, "ctx", "head"), P("head", None), P())
    out_specs = P(("ctx", "head"), None)
    return jax.shard_map(
        per_device, mesh=mesh, in_specs=in_specs, out_specs=out_specs, check_vma=False
    )
```

```python
import jax
import jax.numpy as jnp
from jax import lax
from jax.sharding import PartitionSpec as P

HD = 128
SPAN = 3
DOC_MOST = 1152
CHUNK = 128


def shift_up(x, axis):
    peers = lax.axis_size(axis)
    return lax.ppermute(x, axis, [(i, i + 1) for i in range(peers - 1)])


def rotate(x, axis, by):
    peers = lax.axis_size(axis)
    return lax.ppermute(x, axis, [(i, (i + by) % peers) for i in range(peers)])


def per_device(queries, keys_values, w_out, doc_index):
    rows, width = queries.shape
    heads = width // HD
    groups = lax.axis_size("head")
    me = lax.axis_index("ctx")
    h = lax.axis_index("head")
    first_row = me * rows
    tail = DOC_MOST - 2 * rows
    keys, values = keys_values[0], keys_values[1]
    r1 = (shift_up(keys, "ctx"), shift_up(values, "ctx"))
    r2 = tuple(shift_up(x, "ctx") for x in r1)
    r3 = tuple(shift_up(x[rows - tail:], "ctx") for x in r2)
    sources = [r3, r2, r1, (keys, values)]
    offsets = [-DOC_MOST, -2 * rows, -rows, 0]
    padded_docs = jnp.concatenate([jnp.full((DOC_MOST,), -1, jnp.int32), doc_index])
    scale = HD ** (-0.5)

    def chunk_part(c):
        start = c * CHUNK
        q = lax.dynamic_slice_in_dim(queries, start, CHUNK, 0).reshape(CHUNK, heads, HD)
        q_docs = lax.dynamic_slice_in_dim(doc_index, first_row + start, CHUNK)
        q_place = start + jnp.arange(CHUNK, dtype=jnp.int32)
        def scores(kv, off):
            n = kv[0].shape[0]
            k = kv[0].reshape(n, heads, HD)
            k_docs = lax.dynamic_slice_in_dim(padded_docs, first_row + DOC_MOST + off, n)
            k_place = off + jnp.arange(n, dtype=jnp.int32)
            allowed = (k_docs[None, :] == q_docs[:, None]) & (k_place[None, :] <= q_place[:, None])
            raw = jnp.einsum("qhd,khd->hqk", q, k, preferred_element_type=jnp.float32) * scale
            return jnp.where(allowed[None], raw, jnp.float32(-1e30))

        def stage(pairs, top):
            score_list = [scores(kv, off) for kv, off in pairs]
            for s in score_list:
                top = jnp.maximum(top, s.max(axis=2, keepdims=True))
            total = None
            summed = None
            for (kv, _), s in zip(pairs, score_list):
                n = kv[0].shape[0]
                weights = jnp.exp(s - top)
                t = jnp.sum(weights, axis=2)
                probs = weights.astype(jnp.bfloat16)
                pv = jnp.einsum("hqk,khd->qhd", probs, kv[1].reshape(n, heads, HD), preferred_element_type=jnp.float32)
                total = t if total is None else total + t
                summed = pv if summed is None else summed + pv
            return top, total, summed

        near = list(zip(sources[2:], offsets[2:]))
        far = list(zip(sources[:2], offsets[:2]))
        floor = jnp.full((heads, CHUNK, 1), -1e30, jnp.float32)
        top_a, total_a, summed_a = stage(near, floor)
        top, total_b, summed_b = stage(far, top_a)
        alpha = jnp.exp(top_a - top)
        total = alpha[:, :, 0] * total_a + total_b
        summed = jnp.transpose(alpha, (1, 0, 2)) * summed_a + summed_b
        attended = (summed / jnp.transpose(total)[:, :, None]).astype(jnp.bfloat16)
        attended = attended.reshape(CHUNK, heads * HD)
        return jnp.dot(attended, w_out, preferred_element_type=jnp.float32).astype(jnp.bfloat16)

    assert groups == 4
    cols = w_out.shape[1] // 2
    far = chunk_part((h + 2) % groups)
    via_left = rotate(far[:, :cols], "head", groups - 1)
    via_right = rotate(far[:, cols:], "head", 1)
    nxt = chunk_part((h + 1) % groups)
    nxt = jnp.concatenate(
        [nxt[:, :cols], (nxt[:, cols:].astype(jnp.float32) + via_right.astype(jnp.float32)).astype(jnp.bfloat16)],
        axis=1,
    )
    from_left = rotate(nxt, "head", 1)
    prv = chunk_part((h + groups - 1) % groups)
    prv = jnp.concatenate(
        [(prv[:, :cols].astype(jnp.float32) + via_left.astype(jnp.float32)).astype(jnp.bfloat16), prv[:, cols:]],
        axis=1,
    )
    from_right = rotate(prv, "head", groups - 1)
    own = chunk_part(h)
    total_out = own.astype(jnp.float32) + from_left.astype(jnp.float32) + from_right.astype(jnp.float32)
    return total_out.astype(jnp.bfloat16)


def solution(mesh):
    in_specs = (P("ctx", "head"), P(None, "ctx", "head"), P("head", None), P())
    out_specs = P(("ctx", "head"), None)
    return jax.shard_map(
        per_device, mesh=mesh, in_specs=in_specs, out_specs=out_specs, check_vma=False
    )
```

```python
import jax
import jax.numpy as jnp
from jax import lax
from jax.sharding import PartitionSpec as P

HD = 128
SPAN = 3
DOC_MOST = 1152
CHUNK = 128


def shift_up(x, axis):
    peers = lax.axis_size(axis)
    return lax.ppermute(x, axis, [(i, i + 1) for i in range(peers - 1)])


def rotate(x, axis, by):
    peers = lax.axis_size(axis)
    return lax.ppermute(x, axis, [(i, (i + by) % peers) for i in range(peers)])


def per_device(queries, keys_values, w_out, doc_index):
    rows, width = queries.shape
    heads = width // HD
    groups = lax.axis_size("head")
    me = lax.axis_index("ctx")
    h = lax.axis_index("head")
    first_row = me * rows
    tail = DOC_MOST - 2 * rows
    r1 = shift_up(keys_values, "ctx")
    r2 = shift_up(r1, "ctx")
    sources = [None, r2, r1, keys_values]
    offsets = [-DOC_MOST, -2 * rows, -rows, 0]
    padded_docs = jnp.concatenate([jnp.full((DOC_MOST,), -1, jnp.int32), doc_index])
    scale = HD ** (-0.5)

    def chunk_state(c, upto):
        start = c * CHUNK
        q = lax.dynamic_slice_in_dim(queries, start, CHUNK, 0).reshape(CHUNK, heads, HD)
        q_docs = lax.dynamic_slice_in_dim(doc_index, first_row + start, CHUNK)
        q_place = start + jnp.arange(CHUNK, dtype=jnp.int32)

        def scores(kv, off):
            n = kv.shape[1]
            k = kv[0].reshape(n, heads, HD)
            k_docs = lax.dynamic_slice_in_dim(padded_docs, first_row + DOC_MOST + off, n)
            k_place = off + jnp.arange(n, dtype=jnp.int32)
            allowed = (k_docs[None, :] == q_docs[:, None]) & (k_place[None, :] <= q_place[:, None])
            raw = jnp.einsum("qhd,khd->hqk", q, k, preferred_element_type=jnp.float32) * scale
            return jnp.where(allowed[None], raw, jnp.float32(-1e30))

        def stage(pairs, top):
            score_list = [scores(kv, off) for kv, off in pairs]
            for s in score_list:
                top = jnp.maximum(top, s.max(axis=2, keepdims=True))
            total = None
            summed = None
            for (kv, _), s in zip(pairs, score_list):
                n = kv.shape[1]
                weights = jnp.exp(s - top)
                t = jnp.sum(weights, axis=2)
                probs = weights.astype(jnp.bfloat16)
                pv = jnp.einsum("hqk,khd->qhd", probs, kv[1].reshape(n, heads, HD), preferred_element_type=jnp.float32)
                total = t if total is None else total + t
                summed = pv if summed is None else summed + pv
            return top, total, summed

        def fold(state, kv, off):
            top, total, summed = state
            new_top, new_total, new_summed = stage([(kv, off)], top)
            alpha = jnp.exp(top - new_top)
            total = alpha[:, :, 0] * total + new_total
            summed = jnp.transpose(alpha, (1, 0, 2)) * summed + new_summed
            return new_top, total, summed

        floor = jnp.full((heads, CHUNK, 1), -1e30, jnp.float32)
        state = stage(list(zip(sources[2:], offsets[2:])), floor)
        for kv, off in upto:
            state = fold(state, kv, off)
        return state, fold

    def finish(state):
        top, total, summed = state
        attended = (summed / jnp.transpose(total)[:, :, None]).astype(jnp.bfloat16)
        attended = attended.reshape(CHUNK, heads * HD)
        return jnp.dot(attended, w_out, preferred_element_type=jnp.float32).astype(jnp.bfloat16)

    def chunk_part(c):
        state, fold = chunk_state(c, [(r2, offsets[1])])
        return finish(fold(state, r3, offsets[0]))

    assert groups == 4
    cols = w_out.shape[1] // 2
    far_state, fold = chunk_state((h + 2) % groups, [(r2, offsets[1])])
    relay, far_state = lax.optimization_barrier((r2[:, rows - tail:], far_state))
    r3 = shift_up(relay, "ctx")
    far = finish(fold(far_state, r3, offsets[0]))
    via_left = rotate(far[:, :cols], "head", groups - 1)
    via_right = rotate(far[:, cols:], "head", 1)
    nxt = chunk_part((h + 1) % groups)
    nxt = jnp.concatenate(
        [nxt[:, :cols], (nxt[:, cols:].astype(jnp.float32) + via_right.astype(jnp.float32)).astype(jnp.bfloat16)],
        axis=1,
    )
    from_left = rotate(nxt, "head", 1)
    prv = chunk_part((h + groups - 1) % groups)
    prv = jnp.concatenate(
        [(prv[:, :cols].astype(jnp.float32) + via_left.astype(jnp.float32)).astype(jnp.bfloat16), prv[:, cols:]],
        axis=1,
    )
    from_right = rotate(prv, "head", groups - 1)
    own = chunk_part(h)
    total_out = own.astype(jnp.float32) + from_left.astype(jnp.float32) + from_right.astype(jnp.float32)
    return total_out.astype(jnp.bfloat16)


def solution(mesh):
    in_specs = (P("ctx", "head"), P(None, "ctx", "head"), P("head", None), P())
    out_specs = P(("ctx", "head"), None)
    return jax.shard_map(
        per_device, mesh=mesh, in_specs=in_specs, out_specs=out_specs, check_vma=False
    )
```

```python
import jax
import jax.numpy as jnp
from jax import lax
from jax.experimental.layout import Layout, with_layout_constraint
from jax.sharding import PartitionSpec as P

HD = 128
SPAN = 3
DOC_MOST = 1152
CHUNK = 128


def shift_up(x, axis):
    peers = lax.axis_size(axis)
    return lax.ppermute(x, axis, [(i, i + 1) for i in range(peers - 1)])


def rotate(x, axis, by):
    peers = lax.axis_size(axis)
    return lax.ppermute(x, axis, [(i, (i + by) % peers) for i in range(peers)])


def per_device(queries, keys_values, w_out, doc_index):
    rows, width = queries.shape
    heads = width // HD
    groups = lax.axis_size("head")
    me = lax.axis_index("ctx")
    h = lax.axis_index("head")
    first_row = me * rows
    tail = DOC_MOST - 2 * rows
    def relay(x):
        x = with_layout_constraint(x, Layout(major_to_minor=(0, 1, 2)))
        return with_layout_constraint(shift_up(x, "ctx"), Layout(major_to_minor=(0, 1, 2)))

    r1 = relay(keys_values)
    r2 = relay(r1)
    r3 = relay(r2[:, rows - tail:])
    sources = [r3, r2, r1, keys_values]
    offsets = [-DOC_MOST, -2 * rows, -rows, 0]
    padded_docs = jnp.concatenate([jnp.full((DOC_MOST,), -1, jnp.int32), doc_index])
    scale = HD ** (-0.5)

    def chunk_part(c):
        start = c * CHUNK
        q = lax.dynamic_slice_in_dim(queries, start, CHUNK, 0).reshape(CHUNK, heads, HD)
        q_docs = lax.dynamic_slice_in_dim(doc_index, first_row + start, CHUNK)
        q_place = start + jnp.arange(CHUNK, dtype=jnp.int32)
        def scores(kv, off):
            n = kv.shape[1]
            k = kv[0].reshape(n, heads, HD)
            k_docs = lax.dynamic_slice_in_dim(padded_docs, first_row + DOC_MOST + off, n)
            k_place = off + jnp.arange(n, dtype=jnp.int32)
            allowed = (k_docs[None, :] == q_docs[:, None]) & (k_place[None, :] <= q_place[:, None])
            raw = jnp.einsum("qhd,khd->hqk", q, k, preferred_element_type=jnp.float32) * scale
            return jnp.where(allowed[None], raw, jnp.float32(-1e30))

        def stage(pairs, top):
            score_list = [scores(kv, off) for kv, off in pairs]
            for s in score_list:
                top = jnp.maximum(top, s.max(axis=2, keepdims=True))
            total = None
            summed = None
            for (kv, _), s in zip(pairs, score_list):
                n = kv.shape[1]
                weights = jnp.exp(s - top)
                t = jnp.sum(weights, axis=2)
                probs = weights.astype(jnp.bfloat16)
                pv = jnp.einsum("hqk,khd->qhd", probs, kv[1].reshape(n, heads, HD), preferred_element_type=jnp.float32)
                total = t if total is None else total + t
                summed = pv if summed is None else summed + pv
            return top, total, summed

        near = list(zip(sources[2:], offsets[2:]))
        far = list(zip(sources[:2], offsets[:2]))
        floor = jnp.full((heads, CHUNK, 1), -1e30, jnp.float32)
        top_a, total_a, summed_a = stage(near, floor)
        top, total_b, summed_b = stage(far, top_a)
        alpha = jnp.exp(top_a - top)
        total = alpha[:, :, 0] * total_a + total_b
        summed = jnp.transpose(alpha, (1, 0, 2)) * summed_a + summed_b
        attended = (summed / jnp.transpose(total)[:, :, None]).astype(jnp.bfloat16)
        attended = attended.reshape(CHUNK, heads * HD)
        return jnp.dot(attended, w_out, preferred_element_type=jnp.float32).astype(jnp.bfloat16)

    assert groups == 4
    cols = w_out.shape[1] // 2
    far = chunk_part((h + 2) % groups)
    via_left = rotate(far[:, :cols], "head", groups - 1)
    via_right = rotate(far[:, cols:], "head", 1)
    nxt = chunk_part((h + 1) % groups)
    nxt = jnp.concatenate(
        [nxt[:, :cols], (nxt[:, cols:].astype(jnp.float32) + via_right.astype(jnp.float32)).astype(jnp.bfloat16)],
        axis=1,
    )
    from_left = rotate(nxt, "head", 1)
    prv = chunk_part((h + groups - 1) % groups)
    prv = jnp.concatenate(
        [(prv[:, :cols].astype(jnp.float32) + via_left.astype(jnp.float32)).astype(jnp.bfloat16), prv[:, cols:]],
        axis=1,
    )
    from_right = rotate(prv, "head", groups - 1)
    own = chunk_part(h)
    total_out = own.astype(jnp.float32) + from_left.astype(jnp.float32) + from_right.astype(jnp.float32)
    return total_out.astype(jnp.bfloat16)


def solution(mesh):
    in_specs = (P("ctx", "head"), P(None, "ctx", "head"), P("head", None), P())
    out_specs = P(("ctx", "head"), None)
    return jax.shard_map(
        per_device, mesh=mesh, in_specs=in_specs, out_specs=out_specs, check_vma=False
    )
```

```python
import jax
import jax.numpy as jnp
from jax import lax
from jax.sharding import PartitionSpec as P

HD = 128
SPAN = 3
DOC_MOST = 1152
CHUNK = 128


def shift_up(x, axis):
    peers = lax.axis_size(axis)
    return lax.ppermute(x, axis, [(i, i + 1) for i in range(peers - 1)])


def rotate(x, axis, by):
    peers = lax.axis_size(axis)
    return lax.ppermute(x, axis, [(i, (i + by) % peers) for i in range(peers)])


def per_device(queries, keys_values, w_out, doc_index):
    rows, width = queries.shape
    heads = width // HD
    groups = lax.axis_size("head")
    me = lax.axis_index("ctx")
    h = lax.axis_index("head")
    first_row = me * rows
    tail = DOC_MOST - 2 * rows
    r1 = shift_up(keys_values, "ctx")
    r2 = shift_up(r1, "ctx")
    peers = lax.axis_size("ctx")
    tail_even = lax.ppermute(r1[:, rows - tail:], "ctx", [(i, i + 2) for i in range(0, peers - 2, 2)])
    tail_odd = lax.ppermute(r2[:, rows - tail:], "ctx", [(i, i + 1) for i in range(0, peers - 1, 2)])
    r3 = jnp.where(me % 2 == 0, tail_even, tail_odd)
    sources = [r3, r2, r1, keys_values]
    offsets = [-DOC_MOST, -2 * rows, -rows, 0]
    padded_docs = jnp.concatenate([jnp.full((DOC_MOST,), -1, jnp.int32), doc_index])
    scale = HD ** (-0.5)

    def chunk_part(c):
        start = c * CHUNK
        q = lax.dynamic_slice_in_dim(queries, start, CHUNK, 0).reshape(CHUNK, heads, HD)
        q_docs = lax.dynamic_slice_in_dim(doc_index, first_row + start, CHUNK)
        q_place = start + jnp.arange(CHUNK, dtype=jnp.int32)
        def scores(kv, off):
            n = kv.shape[1]
            k = kv[0].reshape(n, heads, HD)
            k_docs = lax.dynamic_slice_in_dim(padded_docs, first_row + DOC_MOST + off, n)
            k_place = off + jnp.arange(n, dtype=jnp.int32)
            allowed = (k_docs[None, :] == q_docs[:, None]) & (k_place[None, :] <= q_place[:, None])
            raw = jnp.einsum("qhd,khd->hqk", q, k, preferred_element_type=jnp.float32) * scale
            return jnp.where(allowed[None], raw, jnp.float32(-1e30))

        def stage(pairs, top):
            score_list = [scores(kv, off) for kv, off in pairs]
            for s in score_list:
                top = jnp.maximum(top, s.max(axis=2, keepdims=True))
            total = None
            summed = None
            for (kv, _), s in zip(pairs, score_list):
                n = kv.shape[1]
                weights = jnp.exp(s - top)
                t = jnp.sum(weights, axis=2)
                probs = weights.astype(jnp.bfloat16)
                pv = jnp.einsum("hqk,khd->qhd", probs, kv[1].reshape(n, heads, HD), preferred_element_type=jnp.float32)
                total = t if total is None else total + t
                summed = pv if summed is None else summed + pv
            return top, total, summed

        near = list(zip(sources[2:], offsets[2:]))
        far = list(zip(sources[:2], offsets[:2]))
        floor = jnp.full((heads, CHUNK, 1), -1e30, jnp.float32)
        top_a, total_a, summed_a = stage(near, floor)
        top, total_b, summed_b = stage(far, top_a)
        alpha = jnp.exp(top_a - top)
        total = alpha[:, :, 0] * total_a + total_b
        summed = jnp.transpose(alpha, (1, 0, 2)) * summed_a + summed_b
        attended = (summed / jnp.transpose(total)[:, :, None]).astype(jnp.bfloat16)
        attended = attended.reshape(CHUNK, heads * HD)
        return jnp.dot(attended, w_out, preferred_element_type=jnp.float32).astype(jnp.bfloat16)

    assert groups == 4
    cols = w_out.shape[1] // 2
    far = chunk_part((h + 2) % groups)
    via_left = rotate(far[:, :cols], "head", groups - 1)
    via_right = rotate(far[:, cols:], "head", 1)
    nxt = chunk_part((h + 1) % groups)
    nxt = jnp.concatenate(
        [nxt[:, :cols], (nxt[:, cols:].astype(jnp.float32) + via_right.astype(jnp.float32)).astype(jnp.bfloat16)],
        axis=1,
    )
    from_left = rotate(nxt, "head", 1)
    prv = chunk_part((h + groups - 1) % groups)
    prv = jnp.concatenate(
        [(prv[:, :cols].astype(jnp.float32) + via_left.astype(jnp.float32)).astype(jnp.bfloat16), prv[:, cols:]],
        axis=1,
    )
    from_right = rotate(prv, "head", groups - 1)
    own = chunk_part(h)
    total_out = own.astype(jnp.float32) + from_left.astype(jnp.float32) + from_right.astype(jnp.float32)
    return total_out.astype(jnp.bfloat16)


def solution(mesh):
    in_specs = (P("ctx", "head"), P(None, "ctx", "head"), P("head", None), P())
    out_specs = P(("ctx", "head"), None)
    return jax.shard_map(
        per_device, mesh=mesh, in_specs=in_specs, out_specs=out_specs, check_vma=False
    )
```

```python
import jax
import jax.numpy as jnp
from jax import lax
from jax.sharding import PartitionSpec as P

HD = 128
SPAN = 3
DOC_MOST = 1152
CHUNK = 128


def shift_up(x, axis):
    peers = lax.axis_size(axis)
    return lax.ppermute(x, axis, [(i, i + 1) for i in range(peers - 1)])


def rotate(x, axis, by):
    peers = lax.axis_size(axis)
    return lax.ppermute(x, axis, [(i, (i + by) % peers) for i in range(peers)])


def per_device(queries, keys_values, w_out, doc_index):
    rows, width = queries.shape
    heads = width // HD
    groups = lax.axis_size("head")
    me = lax.axis_index("ctx")
    h = lax.axis_index("head")
    first_row = me * rows
    tail = DOC_MOST - 2 * rows
    r1 = shift_up(keys_values, "ctx")
    r2 = shift_up(r1, "ctx")
    peers = lax.axis_size("ctx")
    tail_even = lax.ppermute(r1[:, rows - tail:], "ctx", [(i, i + 2) for i in range(0, peers - 2, 2)])
    tail_odd = lax.ppermute(r2[:, rows - tail:], "ctx", [(i, i + 1) for i in range(0, peers - 1, 2)])
    r3 = jnp.where(me % 2 == 0, tail_even, tail_odd)
    sources = [r3, r2, r1, keys_values]
    offsets = [-DOC_MOST, -2 * rows, -rows, 0]
    padded_docs = jnp.concatenate([jnp.full((DOC_MOST,), -1, jnp.int32), doc_index])
    scale = HD ** (-0.5)

    def chunk_part(c):
        start = c * CHUNK
        q = lax.dynamic_slice_in_dim(queries, start, CHUNK, 0).reshape(CHUNK, heads, HD)
        q_docs = lax.dynamic_slice_in_dim(doc_index, first_row + start, CHUNK)
        q_place = start + jnp.arange(CHUNK, dtype=jnp.int32)
        def scores(kv, off):
            n = kv.shape[1]
            k = kv[0].reshape(n, heads, HD)
            k_docs = lax.dynamic_slice_in_dim(padded_docs, first_row + DOC_MOST + off, n)
            k_place = off + jnp.arange(n, dtype=jnp.int32)
            allowed = (k_docs[None, :] == q_docs[:, None]) & (k_place[None, :] <= q_place[:, None])
            raw = jnp.einsum("qhd,khd->hqk", q, k, preferred_element_type=jnp.float32) * scale
            return jnp.where(allowed[None], raw, jnp.float32(-1e30))

        def stage(pairs, top):
            score_list = [scores(kv, off) for kv, off in pairs]
            for s in score_list:
                top = jnp.maximum(top, s.max(axis=2, keepdims=True))
            total = None
            summed = None
            for (kv, _), s in zip(pairs, score_list):
                n = kv.shape[1]
                weights = jnp.exp(s - top)
                t = jnp.sum(weights, axis=2)
                probs = weights.astype(jnp.bfloat16)
                pv = jnp.einsum("hqk,khd->qhd", probs, kv[1].reshape(n, heads, HD), preferred_element_type=jnp.float32)
                total = t if total is None else total + t
                summed = pv if summed is None else summed + pv
            return top, total, summed

        floor = jnp.full((heads, CHUNK, 1), -1e30, jnp.float32)
        top, total, summed = stage(list(zip(sources[2:], offsets[2:])), floor)
        for kv, off in zip(sources[1::-1], offsets[1::-1]):
            new_top, new_total, new_summed = stage([(kv, off)], top)
            alpha = jnp.exp(top - new_top)
            total = alpha[:, :, 0] * total + new_total
            summed = jnp.transpose(alpha, (1, 0, 2)) * summed + new_summed
            top = new_top
        attended = (summed / jnp.transpose(total)[:, :, None]).astype(jnp.bfloat16)
        attended = attended.reshape(CHUNK, heads * HD)
        return jnp.dot(attended, w_out, preferred_element_type=jnp.float32).astype(jnp.bfloat16)

    assert groups == 4
    cols = w_out.shape[1] // 2
    far = chunk_part((h + 2) % groups)
    via_left = rotate(far[:, :cols], "head", groups - 1)
    via_right = rotate(far[:, cols:], "head", 1)
    nxt = chunk_part((h + 1) % groups)
    nxt = jnp.concatenate(
        [nxt[:, :cols], (nxt[:, cols:].astype(jnp.float32) + via_right.astype(jnp.float32)).astype(jnp.bfloat16)],
        axis=1,
    )
    from_left = rotate(nxt, "head", 1)
    prv = chunk_part((h + groups - 1) % groups)
    prv = jnp.concatenate(
        [(prv[:, :cols].astype(jnp.float32) + via_left.astype(jnp.float32)).astype(jnp.bfloat16), prv[:, cols:]],
        axis=1,
    )
    from_right = rotate(prv, "head", groups - 1)
    own = chunk_part(h)
    total_out = own.astype(jnp.float32) + from_left.astype(jnp.float32) + from_right.astype(jnp.float32)
    return total_out.astype(jnp.bfloat16)


def solution(mesh):
    in_specs = (P("ctx", "head"), P(None, "ctx", "head"), P("head", None), P())
    out_specs = P(("ctx", "head"), None)
    return jax.shard_map(
        per_device, mesh=mesh, in_specs=in_specs, out_specs=out_specs, check_vma=False
    )
```

```python
import jax
import jax.numpy as jnp
from jax import lax
from jax.sharding import PartitionSpec as P

HD = 128
SPAN = 3
DOC_MOST = 1152
CHUNK = 128


def shift_up(x, axis):
    peers = lax.axis_size(axis)
    return lax.ppermute(x, axis, [(i, i + 1) for i in range(peers - 1)])


def rotate(x, axis, by):
    peers = lax.axis_size(axis)
    return lax.ppermute(x, axis, [(i, (i + by) % peers) for i in range(peers)])


def per_device(queries, keys_values, w_out, doc_index):
    rows, width = queries.shape
    heads = width // HD
    groups = lax.axis_size("head")
    me = lax.axis_index("ctx")
    h = lax.axis_index("head")
    first_row = me * rows
    tail = DOC_MOST - 2 * rows
    r1 = shift_up(keys_values, "ctx")
    r2 = shift_up(r1, "ctx")
    peers = lax.axis_size("ctx")
    tail_even = lax.ppermute(r1[:, rows - tail:], "ctx", [(i, i + 2) for i in range(0, peers - 2, 2)])
    tail_odd = lax.ppermute(r2[:, rows - tail:], "ctx", [(i, i + 1) for i in range(0, peers - 1, 2)])
    r3 = jnp.where(me % 2 == 0, tail_even, tail_odd)
    sources = [r3, r2, r1, keys_values]
    offsets = [-DOC_MOST, -2 * rows, -rows, 0]
    padded_docs = jnp.concatenate([jnp.full((DOC_MOST,), -1, jnp.int32), doc_index])
    scale = HD ** (-0.5)

    def chunk_part(c, split=()):
        start = c * CHUNK
        q = lax.dynamic_slice_in_dim(queries, start, CHUNK, 0).reshape(CHUNK, heads, HD)
        q_docs = lax.dynamic_slice_in_dim(doc_index, first_row + start, CHUNK)
        q_place = start + jnp.arange(CHUNK, dtype=jnp.int32)
        def scores(kv, off):
            n = kv.shape[1]
            k = kv[0].reshape(n, heads, HD)
            k_docs = lax.dynamic_slice_in_dim(padded_docs, first_row + DOC_MOST + off, n)
            k_place = off + jnp.arange(n, dtype=jnp.int32)
            allowed = (k_docs[None, :] == q_docs[:, None]) & (k_place[None, :] <= q_place[:, None])
            raw = jnp.einsum("qhd,khd->hqk", q, k, preferred_element_type=jnp.float32) * scale
            return jnp.where(allowed[None], raw, jnp.float32(-1e30))

        def stage(pairs, top):
            score_list = [scores(kv, off) for kv, off in pairs]
            for s in score_list:
                top = jnp.maximum(top, s.max(axis=2, keepdims=True))
            total = None
            summed = None
            for (kv, _), s in zip(pairs, score_list):
                n = kv.shape[1]
                weights = jnp.exp(s - top)
                t = jnp.sum(weights, axis=2)
                probs = weights.astype(jnp.bfloat16)
                pv = jnp.einsum("hqk,khd->qhd", probs, kv[1].reshape(n, heads, HD), preferred_element_type=jnp.float32)
                total = t if total is None else total + t
                summed = pv if summed is None else summed + pv
            return top, total, summed

        floor = jnp.full((heads, CHUNK, 1), -1e30, jnp.float32)
        top, total, summed = stage(list(zip(sources[2:], offsets[2:])), floor)
        for kv, off in zip(sources[1::-1], offsets[1::-1]):
            new_top, new_total, new_summed = stage([(kv, off)], top)
            alpha = jnp.exp(top - new_top)
            total = alpha[:, :, 0] * total + new_total
            summed = jnp.transpose(alpha, (1, 0, 2)) * summed + new_summed
            top = new_top
        attended = (summed / jnp.transpose(total)[:, :, None]).astype(jnp.bfloat16)
        attended = attended.reshape(CHUNK, heads * HD)
        if split:
            return tuple(
                jnp.dot(attended, w, preferred_element_type=jnp.float32).astype(jnp.bfloat16) for w in split
            )
        return jnp.dot(attended, w_out, preferred_element_type=jnp.float32).astype(jnp.bfloat16)

    assert groups == 4
    cols = w_out.shape[1] // 2
    far_left, far_right = chunk_part((h + 2) % groups, (w_out[:, :cols], w_out[:, cols:]))
    via_left = rotate(far_left, "head", groups - 1)
    via_right = rotate(far_right, "head", 1)
    nxt = chunk_part((h + 1) % groups)
    nxt = jnp.concatenate(
        [nxt[:, :cols], (nxt[:, cols:].astype(jnp.float32) + via_right.astype(jnp.float32)).astype(jnp.bfloat16)],
        axis=1,
    )
    from_left = rotate(nxt, "head", 1)
    prv = chunk_part((h + groups - 1) % groups)
    prv = jnp.concatenate(
        [(prv[:, :cols].astype(jnp.float32) + via_left.astype(jnp.float32)).astype(jnp.bfloat16), prv[:, cols:]],
        axis=1,
    )
    from_right = rotate(prv, "head", groups - 1)
    own = chunk_part(h)
    total_out = own.astype(jnp.float32) + from_left.astype(jnp.float32) + from_right.astype(jnp.float32)
    return total_out.astype(jnp.bfloat16)


def solution(mesh):
    in_specs = (P("ctx", "head"), P(None, "ctx", "head"), P("head", None), P())
    out_specs = P(("ctx", "head"), None)
    return jax.shard_map(
        per_device, mesh=mesh, in_specs=in_specs, out_specs=out_specs, check_vma=False
    )
```

```python
import jax
import jax.numpy as jnp
from jax import lax
from jax.sharding import PartitionSpec as P

HD = 128
SPAN = 3
DOC_MOST = 1152
CHUNK = 128


def shift_up(x, axis):
    peers = lax.axis_size(axis)
    return lax.ppermute(x, axis, [(i, i + 1) for i in range(peers - 1)])


def rotate(x, axis, by):
    peers = lax.axis_size(axis)
    return lax.ppermute(x, axis, [(i, (i + by) % peers) for i in range(peers)])


def per_device(queries, keys_values, w_out, doc_index):
    rows, width = queries.shape
    heads = width // HD
    groups = lax.axis_size("head")
    me = lax.axis_index("ctx")
    h = lax.axis_index("head")
    first_row = me * rows
    tail = DOC_MOST - 2 * rows
    r1 = shift_up(keys_values, "ctx")
    r2 = shift_up(r1, "ctx")
    sources = [None, r2, r1, keys_values]
    offsets = [-DOC_MOST, -2 * rows, -rows, 0]
    padded_docs = jnp.concatenate([jnp.full((DOC_MOST,), -1, jnp.int32), doc_index])
    scale = HD ** (-0.5)

    def chunk_state(c, upto):
        start = c * CHUNK
        q = lax.dynamic_slice_in_dim(queries, start, CHUNK, 0).reshape(CHUNK, heads, HD)
        q_docs = lax.dynamic_slice_in_dim(doc_index, first_row + start, CHUNK)
        q_place = start + jnp.arange(CHUNK, dtype=jnp.int32)

        def scores(kv, off):
            n = kv.shape[1]
            k = kv[0].reshape(n, heads, HD)
            k_docs = lax.dynamic_slice_in_dim(padded_docs, first_row + DOC_MOST + off, n)
            k_place = off + jnp.arange(n, dtype=jnp.int32)
            allowed = (k_docs[None, :] == q_docs[:, None]) & (k_place[None, :] <= q_place[:, None])
            raw = jnp.einsum("qhd,khd->hqk", q, k, preferred_element_type=jnp.float32) * scale
            return jnp.where(allowed[None], raw, jnp.float32(-1e30))

        def stage(pairs, top):
            score_list = [scores(kv, off) for kv, off in pairs]
            for s in score_list:
                top = jnp.maximum(top, s.max(axis=2, keepdims=True))
            total = None
            summed = None
            for (kv, _), s in zip(pairs, score_list):
                n = kv.shape[1]
                weights = jnp.exp(s - top)
                t = jnp.sum(weights, axis=2)
                probs = weights.astype(jnp.bfloat16)
                pv = jnp.einsum("hqk,khd->qhd", probs, kv[1].reshape(n, heads, HD), preferred_element_type=jnp.float32)
                total = t if total is None else total + t
                summed = pv if summed is None else summed + pv
            return top, total, summed

        def fold(state, kv, off):
            top, total, summed = state
            new_top, new_total, new_summed = stage([(kv, off)], top)
            alpha = jnp.exp(top - new_top)
            total = alpha[:, :, 0] * total + new_total
            summed = jnp.transpose(alpha, (1, 0, 2)) * summed + new_summed
            return new_top, total, summed

        floor = jnp.full((heads, CHUNK, 1), -1e30, jnp.float32)
        state = stage(list(zip(sources[2:], offsets[2:])), floor)
        for kv, off in upto:
            state = fold(state, kv, off)
        return state, fold

    def finish(state):
        top, total, summed = state
        attended = (summed / jnp.transpose(total)[:, :, None]).astype(jnp.bfloat16)
        attended = attended.reshape(CHUNK, heads * HD)
        return jnp.dot(attended, w_out, preferred_element_type=jnp.float32).astype(jnp.bfloat16)

    def chunk_part(c):
        state, fold = chunk_state(c, [(r2, offsets[1])])
        return finish(fold(state, r3, offsets[0]))

    assert groups == 4
    cols = w_out.shape[1] // 2
    far_state, fold = chunk_state((h + 2) % groups, [(r2, offsets[1])])
    peers = lax.axis_size("ctx")
    tail_even = lax.ppermute(r1[:, rows - tail:], "ctx", [(i, i + 2) for i in range(0, peers - 2, 2)])
    relay, far_state = lax.optimization_barrier((r2[:, rows - tail:], far_state))
    tail_odd = lax.ppermute(relay, "ctx", [(i, i + 1) for i in range(0, peers - 1, 2)])
    r3 = jnp.where(me % 2 == 0, tail_even, tail_odd)
    far = finish(fold(far_state, r3, offsets[0]))
    via_left = rotate(far[:, :cols], "head", groups - 1)
    via_right = rotate(far[:, cols:], "head", 1)
    nxt = chunk_part((h + 1) % groups)
    nxt = jnp.concatenate(
        [nxt[:, :cols], (nxt[:, cols:].astype(jnp.float32) + via_right.astype(jnp.float32)).astype(jnp.bfloat16)],
        axis=1,
    )
    from_left = rotate(nxt, "head", 1)
    prv = chunk_part((h + groups - 1) % groups)
    prv = jnp.concatenate(
        [(prv[:, :cols].astype(jnp.float32) + via_left.astype(jnp.float32)).astype(jnp.bfloat16), prv[:, cols:]],
        axis=1,
    )
    from_right = rotate(prv, "head", groups - 1)
    own = chunk_part(h)
    total_out = own.astype(jnp.float32) + from_left.astype(jnp.float32) + from_right.astype(jnp.float32)
    return total_out.astype(jnp.bfloat16)


def solution(mesh):
    in_specs = (P("ctx", "head"), P(None, "ctx", "head"), P("head", None), P())
    out_specs = P(("ctx", "head"), None)
    return jax.shard_map(
        per_device, mesh=mesh, in_specs=in_specs, out_specs=out_specs, check_vma=False
    )
```

```python
import jax
import jax.numpy as jnp
from jax import lax
from jax.sharding import PartitionSpec as P

HD = 128
SPAN = 3
DOC_MOST = 1152
CHUNK = 128


def shift_up(x, axis):
    peers = lax.axis_size(axis)
    return lax.ppermute(x, axis, [(i, i + 1) for i in range(peers - 1)])


def rotate(x, axis, by):
    peers = lax.axis_size(axis)
    return lax.ppermute(x, axis, [(i, (i + by) % peers) for i in range(peers)])


def per_device(queries, keys_values, w_out, doc_index):
    rows, width = queries.shape
    heads = width // HD
    groups = lax.axis_size("head")
    me = lax.axis_index("ctx")
    h = lax.axis_index("head")
    first_row = me * rows
    tail = DOC_MOST - 2 * rows
    r1 = shift_up(keys_values, "ctx")
    r2 = shift_up(r1, "ctx")
    peers = lax.axis_size("ctx")
    tail_even = lax.ppermute(r1[:, rows - tail:], "ctx", [(i, i + 2) for i in range(0, peers - 2, 2)])
    tail_odd = lax.ppermute(r2[:, rows - tail:], "ctx", [(i, i + 1) for i in range(0, peers - 1, 2)])
    r3 = jnp.where(me % 2 == 0, tail_even, tail_odd)
    sources = [r3, r2, r1, keys_values]
    offsets = [-DOC_MOST, -2 * rows, -rows, 0]
    padded_docs = jnp.concatenate([jnp.full((DOC_MOST,), -1, jnp.int32), doc_index])
    scale = HD ** (-0.5)

    def chunk_part(c):
        start = c * CHUNK
        q = lax.dynamic_slice_in_dim(queries, start, CHUNK, 0).reshape(CHUNK, heads, HD)
        q_docs = lax.dynamic_slice_in_dim(doc_index, first_row + start, CHUNK)
        q_place = start + jnp.arange(CHUNK, dtype=jnp.int32)
        def scores(kv, off):
            n = kv.shape[1]
            k = kv[0].reshape(n, heads, HD)
            k_docs = lax.dynamic_slice_in_dim(padded_docs, first_row + DOC_MOST + off, n)
            k_place = off + jnp.arange(n, dtype=jnp.int32)
            allowed = (k_docs[None, :] == q_docs[:, None]) & (k_place[None, :] <= q_place[:, None])
            raw = jnp.einsum("qhd,khd->hqk", q, k, preferred_element_type=jnp.float32) * scale
            return jnp.where(allowed[None], raw, jnp.float32(-1e30))

        def stage(pairs, top):
            score_list = [scores(kv, off) for kv, off in pairs]
            for s in score_list:
                top = jnp.maximum(top, s.max(axis=2, keepdims=True))
            total = None
            summed = None
            for (kv, _), s in zip(pairs, score_list):
                n = kv.shape[1]
                weights = jnp.exp(s - top)
                t = jnp.sum(weights, axis=2)
                probs = weights.astype(jnp.bfloat16)
                pv = jnp.einsum("hqk,khd->qhd", probs, kv[1].reshape(n, heads, HD), preferred_element_type=jnp.float32)
                total = t if total is None else total + t
                summed = pv if summed is None else summed + pv
            return top, total, summed

        near = list(zip(sources[1:], offsets[1:]))
        far = list(zip(sources[:1], offsets[:1]))
        floor = jnp.full((heads, CHUNK, 1), -1e30, jnp.float32)
        top_a, total_a, summed_a = stage(near, floor)
        top, total_b, summed_b = stage(far, top_a)
        alpha = jnp.exp(top_a - top)
        total = alpha[:, :, 0] * total_a + total_b
        summed = jnp.transpose(alpha, (1, 0, 2)) * summed_a + summed_b
        attended = (summed / jnp.transpose(total)[:, :, None]).astype(jnp.bfloat16)
        attended = attended.reshape(CHUNK, heads * HD)
        return jnp.dot(attended, w_out, preferred_element_type=jnp.float32).astype(jnp.bfloat16)

    assert groups == 4
    cols = w_out.shape[1] // 2
    far = chunk_part((h + 2) % groups)
    via_left = rotate(far[:, :cols], "head", groups - 1)
    via_right = rotate(far[:, cols:], "head", 1)
    nxt = chunk_part((h + 1) % groups)
    nxt = jnp.concatenate(
        [nxt[:, :cols], (nxt[:, cols:].astype(jnp.float32) + via_right.astype(jnp.float32)).astype(jnp.bfloat16)],
        axis=1,
    )
    from_left = rotate(nxt, "head", 1)
    prv = chunk_part((h + groups - 1) % groups)
    prv = jnp.concatenate(
        [(prv[:, :cols].astype(jnp.float32) + via_left.astype(jnp.float32)).astype(jnp.bfloat16), prv[:, cols:]],
        axis=1,
    )
    from_right = rotate(prv, "head", groups - 1)
    own = chunk_part(h)
    total_out = own.astype(jnp.float32) + from_left.astype(jnp.float32) + from_right.astype(jnp.float32)
    return total_out.astype(jnp.bfloat16)


def solution(mesh):
    in_specs = (P("ctx", "head"), P(None, "ctx", "head"), P("head", None), P())
    out_specs = P(("ctx", "head"), None)
    return jax.shard_map(
        per_device, mesh=mesh, in_specs=in_specs, out_specs=out_specs, check_vma=False
    )
```

```python
import jax
import jax.numpy as jnp
from jax import lax
from jax.sharding import PartitionSpec as P

HD = 128
SPAN = 3
DOC_MOST = 1152
CHUNK = 128


def shift_up(x, axis):
    peers = lax.axis_size(axis)
    return lax.ppermute(x, axis, [(i, i + 1) for i in range(peers - 1)])


def rotate(x, axis, by):
    peers = lax.axis_size(axis)
    return lax.ppermute(x, axis, [(i, (i + by) % peers) for i in range(peers)])


def per_device(queries, keys_values, w_out, doc_index):
    rows, width = queries.shape
    heads = width // HD
    groups = lax.axis_size("head")
    me = lax.axis_index("ctx")
    h = lax.axis_index("head")
    first_row = me * rows
    tail = DOC_MOST - 2 * rows
    r1 = shift_up(keys_values, "ctx")
    r2 = shift_up(r1, "ctx")
    peers = lax.axis_size("ctx")
    tail_even = lax.ppermute(r1[:, rows - tail:], "ctx", [(i, i + 2) for i in range(0, peers - 2, 2)])
    tail_odd = lax.ppermute(r2[:, rows - tail:], "ctx", [(i, i + 1) for i in range(0, peers - 1, 2)])
    r3 = jnp.where(me % 2 == 0, tail_even, tail_odd)
    sources = [r3, r2, r1, keys_values]
    offsets = [-DOC_MOST, -2 * rows, -rows, 0]
    padded_docs = jnp.concatenate([jnp.full((DOC_MOST,), -1, jnp.int32), doc_index])
    scale = HD ** (-0.5)

    def chunk_part(c):
        start = c * CHUNK
        q = lax.dynamic_slice_in_dim(queries, start, CHUNK, 0).reshape(CHUNK, heads, HD)
        q_docs = lax.dynamic_slice_in_dim(doc_index, first_row + start, CHUNK)
        q_place = start + jnp.arange(CHUNK, dtype=jnp.int32)
        def scores(kv, off):
            n = kv.shape[1]
            k = kv[0].reshape(n, heads, HD)
            k_docs = lax.dynamic_slice_in_dim(padded_docs, first_row + DOC_MOST + off, n)
            k_place = off + jnp.arange(n, dtype=jnp.int32)
            allowed = (k_docs[None, :] == q_docs[:, None]) & (k_place[None, :] <= q_place[:, None])
            raw = jnp.einsum("khd,qhd->hkq", k, q, preferred_element_type=jnp.float32) * scale
            return jnp.where(jnp.transpose(allowed)[None], raw, jnp.float32(-1e30))

        def stage(pairs, top):
            score_list = [scores(kv, off) for kv, off in pairs]
            for s in score_list:
                top = jnp.maximum(top, s.max(axis=1, keepdims=True))
            total = None
            summed = None
            for (kv, _), s in zip(pairs, score_list):
                n = kv.shape[1]
                weights = jnp.exp(s - top)
                t = jnp.sum(weights, axis=1)
                probs = weights.astype(jnp.bfloat16)
                pv = jnp.einsum("hkq,khd->qhd", probs, kv[1].reshape(n, heads, HD), preferred_element_type=jnp.float32)
                total = t if total is None else total + t
                summed = pv if summed is None else summed + pv
            return top, total, summed

        near = list(zip(sources[2:], offsets[2:]))
        far = list(zip(sources[:2], offsets[:2]))
        floor = jnp.full((heads, 1, CHUNK), -1e30, jnp.float32)
        top_a, total_a, summed_a = stage(near, floor)
        top, total_b, summed_b = stage(far, top_a)
        alpha = jnp.exp(top_a - top)
        total = alpha[:, 0, :] * total_a + total_b
        summed = jnp.transpose(alpha, (2, 0, 1)) * summed_a + summed_b
        attended = (summed / jnp.transpose(total)[:, :, None]).astype(jnp.bfloat16)
        attended = attended.reshape(CHUNK, heads * HD)
        return jnp.dot(attended, w_out, preferred_element_type=jnp.float32).astype(jnp.bfloat16)

    assert groups == 4
    cols = w_out.shape[1] // 2
    far = chunk_part((h + 2) % groups)
    via_left = rotate(far[:, :cols], "head", groups - 1)
    via_right = rotate(far[:, cols:], "head", 1)
    nxt = chunk_part((h + 1) % groups)
    nxt = jnp.concatenate(
        [nxt[:, :cols], (nxt[:, cols:].astype(jnp.float32) + via_right.astype(jnp.float32)).astype(jnp.bfloat16)],
        axis=1,
    )
    from_left = rotate(nxt, "head", 1)
    prv = chunk_part((h + groups - 1) % groups)
    prv = jnp.concatenate(
        [(prv[:, :cols].astype(jnp.float32) + via_left.astype(jnp.float32)).astype(jnp.bfloat16), prv[:, cols:]],
        axis=1,
    )
    from_right = rotate(prv, "head", groups - 1)
    own = chunk_part(h)
    total_out = own.astype(jnp.float32) + from_left.astype(jnp.float32) + from_right.astype(jnp.float32)
    return total_out.astype(jnp.bfloat16)


def solution(mesh):
    in_specs = (P("ctx", "head"), P(None, "ctx", "head"), P("head", None), P())
    out_specs = P(("ctx", "head"), None)
    return jax.shard_map(
        per_device, mesh=mesh, in_specs=in_specs, out_specs=out_specs, check_vma=False
    )
```
